32 devices in a mesh: dp: 4 (over y, x), tp: 8 (over z, core).
Axes of the slice: x: 2, y: 2, z: 4, core: 2. Of those that a mesh axis runs over, the one named last changes fastest.
Arguments:
- hidden_in: bfloat16 [4, 32, 4096], P(None, 'dp'), may hold values from -6 to 6
- pre_gain: float32 [4096], replicated, may hold values from 0.25 to 1.75
- w_zx: bfloat16 [4096, 2, 8192], P(None, None, 'tp'), may hold values from -0.09375 to 0.09375
- zx_codes: bfloat16 [4096, 2, 8192], P(('dp', 'tp')), may hold values from -4 to 4
- zx_exponents: int32 [32, 2, 64], P('dp', None, 'tp'), may hold values from -9 to -6
- w_bc: bfloat16 [4096, 2048], P(None, 'tp'), may hold values from -0.09375 to 0.09375
- w_dt: bfloat16 [4096, 128], P(None, 'tp'), may hold values from -0.09375 to 0.09375
- conv_x: float32 [5, 8192], P(None, 'tp'), may hold values from -0.6 to 0.6
- conv_bc: float32 [5, 2048], P(None, 'tp'), may hold values from -0.6 to 0.6
- dt_bias: float32 [128], P('tp'), may hold values from -2 to 0.5
- decay_rate: float32 [128], P('tp'), may hold values from 0.05 to 2
- skip_gain: float32 [128], P('tp'), may hold values from 0.5 to 1.5
- conv_state_x: bfloat16 [32, 3, 8192], P('dp', None, 'tp'), may hold values from -6 to 6
- conv_state_bc: bfloat16 [32, 3, 2048], P('dp', None, 'tp'), may hold values from -6 to 6
- ssm_state: float32 [32, 128, 64, 256], P('dp', 'tp'), may hold values from -6 to 6
- norm_gain: float32 [8192], P('tp'), may hold values from 0.25 to 1.75
- w_out: bfloat16 [8192, 4096], P('tp'), may hold values from -0.0625 to 0.0625
- out_codes: bfloat16 [8192, 4096], P('tp', 'dp'), may hold values from -4 to 4
- out_exponents: int32 [64, 32], P('tp', 'dp'), may hold values from -7 to -4
Outputs:
- mixed: bfloat16 [4, 32, 4096], P(None, 'dp', 'tp')
- final_state: float32 [32, 128, 64, 256], P('dp', 'tp')
The draws below stay inside these ranges and needn't reach their ends.
All inputs are finite; a program needn't handle non-finite values.
Results may differ from the reference program's by a relative error of at most 0.014.
Values may be sent and summed in bfloat16 or wider, within the bound.
A program may use at most 192 MiB of HBM per device.

```python
import math
import jax
import jax.numpy as jnp
from jax import lax

D = 4096
H = 128
P_SIZE = 64
N = 256
G = 4
BLK = 128
STEPS = 4
DI = 8192
ROWS = 32


def set_ends(drawn, own_key, smallest, top_value):
    longest = drawn.shape.index(max(drawn.shape))
    spots = []
    for shift in (0, 1):
        where = [jax.random.randint(jax.random.fold_in(own_key, axis), (), 0, length) for axis, length in enumerate(drawn.shape)]
        where[longest] = (where[longest] + shift) % drawn.shape[longest]
        spots.append(tuple(where))
    return drawn.at[spots[0]].set(smallest).at[spots[1]].set(top_value)


def block_scale(rng, dims, shards, smallest, top_value):
    loudness, own = 1.0, jax.random.fold_in(rng, 6)
    for dim, blocks in shards:
        draws = jnp.exp(jax.random.uniform(jax.random.fold_in(own, dim), (blocks,), jnp.float32, smallest / len(shards), top_value / len(shards)))
        loudness = loudness * jnp.repeat(draws, dims[dim] // blocks).reshape([-1 if axis == dim else 1 for axis in range(len(dims))])
    return loudness


def bell_draw(own_key, dims, width, bound, split=(), held_as=jnp.bfloat16):
    gain = block_scale(own_key, dims, split, -0.22, 0.18) if split else 1.0
    array = jax.random.normal(own_key, dims, jnp.float32) * width * gain
    return jnp.minimum(jnp.maximum(array, -bound), bound).astype(held_as)


def setup_inputs(seed: int = 0) -> dict:
    seeds = jax.random.split(jax.random.key(seed), 20)
    return {
        "hidden_in": bell_draw(seeds[0], (STEPS, ROWS, D), 1.0, 6.0, ((1, 4),)),
        "pre_gain": jnp.clip(1.0 + 0.15 * jax.random.normal(seeds[1], (D,), jnp.float32), 0.25, 1.75),
        "w_zx": bell_draw(seeds[2], (D, 2, DI), D ** -0.5, 0.09375, ((2, 8),)),
        "zx_codes": bell_draw(seeds[3], (D, 2, DI), 1.0, 4.0, ((0, 32),)),
        "zx_exponents": set_ends(jax.random.randint(seeds[4], (D // BLK, 2, DI // BLK), -9, -5), jax.random.fold_in(seeds[4], 1), -9, (-5) - 1).astype(jnp.int32),
        "w_bc": bell_draw(seeds[5], (D, 2 * G * N), D ** -0.5, 0.09375, ((1, 8),)),
        "w_dt": bell_draw(seeds[6], (D, H), D ** -0.5, 0.09375, ((1, 8),)),
        "conv_x": jnp.clip(jax.random.uniform(seeds[7], (5, DI), jnp.float32, -0.6, 0.6) * block_scale(seeds[7], (5, DI), ((1, 8),), -0.4, 0.0), -0.6, 0.6),
        "conv_bc": jnp.clip(jax.random.uniform(seeds[8], (5, 2 * G * N), jnp.float32, -0.6, 0.6) * block_scale(seeds[8], (5, 2 * G * N), ((1, 8),), -0.4, 0.0), -0.6, 0.6),
        "dt_bias": jnp.clip(-2.0 + 2.5 * jax.random.uniform(seeds[9], (H,), jnp.float32) ** block_scale(seeds[9], (H,), ((0, 8),), -0.2, 0.2), -2.0, 0.5),
        "decay_rate": jnp.clip(jnp.exp(math.log(2.0) - 3.6888794 * jax.random.uniform(seeds[10], (H,), jnp.float32) ** block_scale(seeds[10], (H,), ((0, 8),), -0.2, 0.2)), 0.05, 2.0),
        "skip_gain": jnp.clip(0.5 + 1.0 * jax.random.uniform(seeds[11], (H,), jnp.float32) ** block_scale(seeds[11], (H,), ((0, 8),), -0.2, 0.2), 0.5, 1.5),
        "conv_state_x": bell_draw(seeds[12], (ROWS, 3, DI), 1.0, 6.0, ((0, 4), (2, 8))),
        "conv_state_bc": bell_draw(seeds[13], (ROWS, 3, 2 * G * N), 1.0, 6.0, ((0, 4), (2, 8))),
        "ssm_state": bell_draw(seeds[14], (ROWS, H, P_SIZE, N), 1.0, 6.0, ((0, 4), (1, 8)), jnp.float32),
        "norm_gain": jnp.clip(1.0 + 0.15 * jax.random.normal(seeds[15], (DI,), jnp.float32), 0.25, 1.75),
        "w_out": bell_draw(seeds[16], (DI, D), DI ** -0.5, 0.0625, ((0, 8),)),
        "out_codes": bell_draw(seeds[17], (DI, D), 1.0, 4.0, ((0, 8), (1, 4))),
        "out_exponents": set_ends(jax.random.randint(seeds[18], (DI // BLK, D // BLK), -7, -3), jax.random.fold_in(seeds[18], 1), -7, (-3) - 1).astype(jnp.int32),
    }


EPS = 1e-05

def decode_pairs(codes, exponents, block):
    rows, pair, cols = codes.shape
    blocked = codes.astype(jnp.float32).reshape(rows // block, block, pair, cols // block, block)
    scales = jnp.exp2(exponents.astype(jnp.float32))
    return (blocked * scales[:, None, :, :, None]).reshape(rows, pair, cols)

def decode_matrix(codes, exponents, block):
    rows, cols = codes.shape
    blocked = codes.astype(jnp.float32).reshape(rows // block, block, cols // block, block)
    scales = jnp.exp2(exponents.astype(jnp.float32))
    return (blocked * scales[:, None, :, None]).reshape(rows, cols)

def conv_step(history, fresh, params):
    window = jnp.concatenate([history, fresh[:, None, :]], axis=1)
    mixed = lax.optimization_barrier(jnp.sum(window * params[:4][None], axis=1)) + params[4]
    return (jax.nn.silu(mixed), window[:, 1:])

def reference(hidden_in, pre_gain, w_zx, zx_codes, zx_exponents, w_bc, w_dt, conv_x, conv_bc, dt_bias, decay_rate, skip_gain, conv_state_x, conv_state_bc, ssm_state, norm_gain, w_out, out_codes, out_exponents):
    new_zx = (w_zx.astype(jnp.float32) + decode_pairs(zx_codes, zx_exponents, BLK)).astype(jnp.bfloat16)
    new_out = (w_out.astype(jnp.float32) + decode_matrix(out_codes, out_exponents, BLK)).astype(jnp.bfloat16)
    zx_flat = new_zx.reshape(D, 2 * DI)
    history_x = conv_state_x.astype(jnp.float32)
    history_bc = conv_state_bc.astype(jnp.float32)
    state = ssm_state
    results = []
    for step in range(STEPS):
        x = hidden_in[step].astype(jnp.float32)
        if step > 0:
            x = x + results[-1].astype(jnp.float32)
        rows = x.shape[0]
        normed = (x * lax.rsqrt(lax.optimization_barrier(jnp.mean(x * x, -1, keepdims=True)) + EPS) * pre_gain).astype(jnp.bfloat16)
        zx = jnp.dot(normed, zx_flat, preferred_element_type=jnp.float32).reshape(rows, 2, DI)
        gate = zx[:, 0]
        inner = zx[:, 1]
        bc_raw = jnp.dot(normed, w_bc, preferred_element_type=jnp.float32)
        dt_raw = jnp.dot(normed, w_dt, preferred_element_type=jnp.float32)
        conv_inner, history_x = conv_step(history_x, inner, conv_x)
        conv_state_out, history_bc = conv_step(history_bc, bc_raw, conv_bc)
        b_heads = jnp.repeat(conv_state_out[:, :G * N].reshape(rows, G, N), H // G, axis=1)
        c_heads = jnp.repeat(conv_state_out[:, G * N:].reshape(rows, G, N), H // G, axis=1)
        step_size = jax.nn.softplus(dt_raw + dt_bias)
        decay = jnp.exp(-step_size * decay_rate)
        inner_heads = conv_inner.reshape(rows, H, P_SIZE)
        state = decay[:, :, None, None] * state + (step_size[:, :, None] * inner_heads)[:, :, :, None] * b_heads[:, :, None, :]
        read = jnp.einsum('rhpn,rhn->rhp', state, c_heads, precision=lax.Precision.HIGHEST) + skip_gain[:, None] * inner_heads
        gated = (read.reshape(rows, DI) * jax.nn.silu(gate)).reshape(rows, G, DI // G)
        grouped = gated * lax.rsqrt(lax.optimization_barrier(jnp.mean(gated * gated, -1, keepdims=True)) + EPS)
        scaled = (grouped.reshape(rows, DI) * norm_gain).astype(jnp.bfloat16)
        results.append(jnp.dot(scaled, new_out, preferred_element_type=jnp.float32).astype(jnp.bfloat16))
    return (jnp.stack(results), state)
```

```python
import jax
import jax.numpy as jnp
from jax import lax
from jax.experimental import pallas as pl
from jax.experimental.pallas import tpu as pltpu
from jax.sharding import PartitionSpec as P

G = 4
BLK = 128
LANES = 128
EPS = 1e-05
MESH = pl.DeviceIdType.MESH
F32 = jnp.float32
BF16 = jnp.bfloat16


def decode_pairs(codes, exponents, block):
    rows, pair, cols = codes.shape
    blocked = codes.astype(F32).reshape(rows // block, block, pair, cols // block, block)
    scales = jnp.exp2(exponents.astype(F32))
    return (blocked * scales[:, None, :, :, None]).reshape(rows, pair, cols)


def decode_matrix(codes, exponents, block):
    rows, cols = codes.shape
    blocked = codes.astype(F32).reshape(rows // block, block, cols // block, block)
    scales = jnp.exp2(exponents.astype(F32))
    return (blocked * scales[:, None, :, None]).reshape(rows, cols)


def silu(v):
    return v / (1.0 + jnp.exp(-v))


def make_kernel(ndp, ntp, steps, rows, dc, lc, cb, heads, psize, nstate, gsz, feats, di):
    oc = feats // ntp
    ac = dc // ntp
    nchunk = lc // LANES
    hpc = LANES // psize
    small = cb + LANES

    def kernel(
        hid_ref, gain_ref, wz_ref, ws_ref, wo_ref, convx_ref, convb_ref, dtb_ref, rate_ref,
        skip_ref, ng_ref, hx0_ref, hb0_ref, state_hbm,
        out_ref, state_out,
        state, hx, hb, hrecv, s1, r1, s2, r2, cs, cr, gs, gr, qs, qr, os, orv, ags, agr, ms, mr,
        tbuf, rbuf,
        st_sem, send_sem, h_sem, sem1, sem2, c_sem, g_sem, q_sem, o_sem, a_sem, m_sem,
    ):
        dp = lax.axis_index("dp")
        tp = lax.axis_index("tp")
        pending = []

        def send(src, dst, rsem, d, t):
            copy = pltpu.make_async_remote_copy(
                src_ref=src, dst_ref=dst, send_sem=send_sem, recv_sem=rsem,
                device_id=(d, t), device_id_type=MESH,
            )
            copy.start()
            pending.append(copy)

        def recv(src, dst, rsem):
            pltpu.make_async_remote_copy(
                src_ref=src, dst_ref=dst, send_sem=send_sem, recv_sem=rsem,
                device_id=(dp, tp), device_id_type=MESH,
            ).wait_recv()

        load = pltpu.make_async_copy(state_hbm, state, st_sem)
        load.start()

        barrier = pltpu.get_barrier_semaphore()
        for i in range(ndp):
            for j in range(ntp):
                if i + j > 0:
                    pl.semaphore_signal(
                        barrier, inc=1,
                        device_id=(lax.rem(dp + i, ndp), lax.rem(tp + j, ntp)),
                        device_id_type=MESH,
                    )
        pl.semaphore_wait(barrier, ndp * ntp - 1)

        for k in range(1, ndp):
            peer = lax.rem(dp + k, ndp)
            send(hid_ref.at[peer], hrecv.at[dp], h_sem.at[k], peer, tp)
        hrecv[dp] = hid_ref[dp]
        hx[0:3] = hx0_ref[...].astype(F32)
        hb[0:3] = hb0_ref[...].astype(F32)
        for k in range(1, ndp):
            src = lax.rem(dp + ndp - k, ndp)
            recv(hid_ref.at[src], hrecv.at[src], h_sem.at[k])

        lane = lax.broadcasted_iota(jnp.int32, (rows, LANES), 1)
        lane_all = lax.broadcasted_iota(jnp.int32, (ndp * rows, LANES), 1)
        lane_sq = lax.broadcasted_iota(jnp.int32, (LANES, LANES), 1)
        owner = tp * oc // dc
        half = (tp * oc - owner * dc) // oc
        group = tp // gsz
        member = tp - group * gsz
        carried = None
        for s in range(steps):
            x = jnp.concatenate([hrecv[d, s].astype(F32) for d in range(ndp)], axis=0)
            if s > 0:
                x = x + carried
            ss = jnp.sum(x * x, axis=1, keepdims=True)
            y = (x * gain_ref[...]).astype(BF16)
            p = jnp.dot(y, ws_ref[...], preferred_element_type=F32)
            last = jnp.where(lane_all == LANES - 1, ss, p[:, cb:])
            for d in range(ndp):
                at = slice(d * rows, (d + 1) * rows)
                s1[s, d, :, :cb] = p[at, :cb]
                s1[s, d, :, cb:] = last[at]
            for k in range(1, ndp):
                peer = lax.rem(dp + k, ndp)
                send(s1.at[s, peer], r1.at[s, k], sem1.at[s, k], peer, tp)
            width = min(512, lc)
            for c in range(0, 2 * lc, width):
                p = jnp.dot(y, wz_ref[:, c : c + width], preferred_element_type=F32)
                for d in range(ndp):
                    s2[s, d, :, c : c + width] = p[d * rows : (d + 1) * rows]
            for k in range(1, ndp):
                peer = lax.rem(dp + k, ndp)
                send(s2.at[s, peer], r2.at[s, k], sem2.at[s, k], peer, tp)
            for k in range(1, ndp):
                recv(s1.at[s, 0], r1.at[s, k], sem1.at[s, k])
            total = s1[s, dp]
            for k in range(1, ndp):
                total = total + r1[s, k]
            inv = lax.rsqrt(total[:, small - 1 :] / feats + EPS)
            hb[s + 3] = total[:, :cb] * inv
            mixed = convb_ref[4:5, :]
            for i in range(4):
                mixed = mixed + hb[s + i] * convb_ref[i : i + 1, :]
            piece = silu(mixed)
            cs[s] = piece
            cr[s, tp] = piece
            for k in range(1, ntp):
                send(cs.at[s], cr.at[s, tp], c_sem.at[s, k], dp, lax.rem(tp + k, ntp))
            z = total[:, cb:] * inv + dtb_ref[...]
            dt = jnp.maximum(z, 0.0) + jnp.log1p(jnp.exp(-jnp.abs(z)))
            decay = jnp.exp(-dt * rate_ref[...])

            for k in range(1, ndp):
                recv(s2.at[s, 0], r2.at[s, k], sem2.at[s, k])
            inners = []
            for j in range(nchunk):
                at = slice(lc + j * LANES, lc + (j + 1) * LANES)
                here = slice(j * LANES, (j + 1) * LANES)
                v = s2[s, dp, :, at]
                for k in range(1, ndp):
                    v = v + r2[s, k, :, at]
                hx[s + 3, :, here] = v * inv
                mixed = convx_ref[4:5, here]
                for i in range(4):
                    mixed = mixed + hx[s + i, :, here] * convx_ref[i : i + 1, here]
                inner = silu(mixed)
                inners.append(inner)
                dte = jnp.zeros((rows, LANES), F32)
                dece = jnp.zeros((rows, LANES), F32)
                for i in range(hpc):
                    h = j * hpc + i
                    inside = (lane >= i * psize) & (lane < (i + 1) * psize)
                    dte = jnp.where(inside, dt[:, h : h + 1], dte)
                    dece = jnp.where(inside, decay[:, h : h + 1], dece)
                tbuf[j, :rows] = dte * inner
                tbuf[j, rows:] = dece
            for k in range(1, ntp):
                src = lax.rem(tp + ntp - k, ntp)
                recv(cs.at[s], cr.at[s, src], c_sem.at[s, k])
            per = nstate // cb
            b0 = group * nstate // cb
            bmat = [cr[s, b0 + i] for i in range(per)]
            cmat = [cr[s, G * nstate // cb + b0 + i] for i in range(per)]
            bmat = bmat[0] if per == 1 else jnp.concatenate(bmat, axis=1)
            cmat = cmat[0] if per == 1 else jnp.concatenate(cmat, axis=1)
            if s == 0:
                load.wait()

            @pl.loop(0, nchunk)
            def _(j):
                full = jnp.concatenate(
                    [tbuf[j], jnp.zeros((LANES - 2 * rows, LANES), F32)], axis=0
                )
                flipped = full.T
                acc = jnp.zeros((LANES, LANES), F32)
                for r in range(rows):
                    new = (
                        flipped[:, rows + r : rows + r + 1] * state[r, j]
                        + flipped[:, r : r + 1] * bmat[r : r + 1, :]
                    )
                    state[r, j] = new
                    q = jnp.sum(new * cmat[r : r + 1, :], axis=1, keepdims=True)
                    acc = jnp.where(lane_sq == r, q, acc)
                rbuf[j] = acc.T[:rows]

            if s == steps - 1:
                store = pltpu.make_async_copy(state, state_out, st_sem)
                store.start()
            ss = jnp.zeros((rows, LANES), F32)
            for j in range(nchunk):
                here = slice(j * LANES, (j + 1) * LANES)
                v = s2[s, dp, :, here]
                for k in range(1, ndp):
                    v = v + r2[s, k, :, here]
                gated = (rbuf[j] + skip_ref[:, here] * inners[j]) * silu(v * inv)
                ss = ss + gated * gated
                gs[s, :, here] = (gated * ng_ref[:, here]).astype(BF16)
            qs[s] = jnp.broadcast_to(jnp.sum(ss, axis=1, keepdims=True), (rows, LANES))
            gr[s, dp] = gs[s]
            qr[s, dp, member] = qs[s]
            for k in range(1, ndp):
                send(gs.at[s], gr.at[s, dp], g_sem.at[s, k], lax.rem(dp + k, ndp), tp)
            for k in range(ndp):
                for m in range(gsz):
                    if k + m > 0:
                        send(
                            qs.at[s], qr.at[s, dp, member], q_sem.at[s, k, m],
                            lax.rem(dp + k, ndp), group * gsz + lax.rem(member + m, gsz),
                        )
            for k in range(ndp):
                src = lax.rem(dp + ndp - k, ndp)
                if k > 0:
                    recv(gs.at[s], gr.at[s, src], g_sem.at[s, k])
                for m in range(gsz):
                    if k + m > 0:
                        frm = lax.rem(member + gsz - m, gsz)
                        recv(qs.at[s], qr.at[s, src, frm], q_sem.at[s, k, m])
            every = jnp.concatenate(
                [gr[s, d].astype(F32) for d in range(ndp)], axis=0
            ).astype(BF16)
            scales = []
            for d in range(ndp):
                sq = qr[s, d, 0]
                for m in range(1, gsz):
                    sq = sq + qr[s, d, m]
                scales.append(lax.rsqrt(sq[:, :1] / (di // G) + EPS))
            scale = jnp.concatenate(scales, axis=0)
            width = max(ac, min(256, dc))
            for c in range(0, dc, width):
                p = jnp.dot(every, wo_ref[:, c : c + width], preferred_element_type=F32) * scale
                for i in range(width // ac):
                    os[s, c // ac + i] = p[:, i * ac : (i + 1) * ac]
            for k in range(1, ntp):
                peer = lax.rem(tp + k, ntp)
                send(os.at[s, peer], orv.at[s, k], o_sem.at[s, k], dp, peer)
            for k in range(1, ntp):
                recv(os.at[s, 0], orv.at[s, k], o_sem.at[s, k])
            total = os[s, tp]
            for k in range(1, ntp):
                total = total + orv[s, k]
            total = total.astype(BF16)
            ags[s] = total
            agr[s, tp] = total
            for k in range(1, ntp):
                send(ags.at[s], agr.at[s, tp], a_sem.at[s, k], dp, lax.rem(tp + k, ntp))
            for k in range(1, ntp):
                src = lax.rem(tp + ntp - k, ntp)
                recv(ags.at[s], agr.at[s, src], a_sem.at[s, k])
            carried = jnp.concatenate([agr[s, t].astype(F32) for t in range(ntp)], axis=1)
            picked = carried[:, :oc]
            for i in range(1, dc // oc):
                picked = jnp.where(half == i, carried[:, i * oc : (i + 1) * oc], picked)
            for d in range(ndp):
                ms[s, d] = picked[d * rows : (d + 1) * rows].astype(BF16)

            @pl.when(owner == dp)
            def _():
                for k in range(1, ndp):
                    peer = lax.rem(dp + k, ndp)
                    pltpu.make_async_remote_copy(
                        src_ref=ms.at[s, peer], dst_ref=mr.at[s], send_sem=m_sem.at[s, 0],
                        recv_sem=m_sem.at[s, 1], device_id=(peer, tp), device_id_type=MESH,
                    ).start()

        store.wait()
        for s in range(steps):
            def final(s=s):
                return pltpu.make_async_remote_copy(
                    src_ref=ms.at[s, 0], dst_ref=mr.at[s], send_sem=m_sem.at[s, 0],
                    recv_sem=m_sem.at[s, 1], device_id=(dp, tp), device_id_type=MESH,
                )

            @pl.when(owner == dp)
            def _():
                out_ref[s] = ms[s, dp]
                for k in range(1, ndp):
                    final().wait_send()

            @pl.when(owner != dp)
            def _():
                final().wait_recv()
                out_ref[s] = mr[s]

        for copy in pending:
            copy.wait_send()

    vm = pltpu.VMEM
    scratch = [
        vm((rows, nchunk, LANES, nstate), F32),
        vm((steps + 3, rows, lc), F32),
        vm((steps + 3, rows, cb), F32),
        vm((ndp, steps, rows, dc), BF16),
        vm((steps, ndp, rows, small), F32),
        vm((steps, ndp, rows, small), F32),
        vm((steps, ndp, rows, 2 * lc), F32),
        vm((steps, ndp, rows, 2 * lc), F32),
        vm((steps, rows, cb), F32),
        vm((steps, ntp, rows, cb), F32),
        vm((steps, rows, lc), BF16),
        vm((steps, ndp, rows, lc), BF16),
        vm((steps, rows, LANES), F32),
        vm((steps, ndp, gsz, rows, LANES), F32),
        vm((steps, ntp, ndp * rows, ac), F32),
        vm((steps, ntp, ndp * rows, ac), F32),
        vm((steps, ndp * rows, ac), BF16),
        vm((steps, ntp, ndp * rows, ac), BF16),
        vm((steps, ndp, rows, oc), BF16),
        vm((steps, rows, oc), BF16),
        vm((nchunk, 2 * rows, LANES), F32),
        vm((nchunk, rows, LANES), F32),
        pltpu.SemaphoreType.DMA(()),
        pltpu.SemaphoreType.DMA(()),
        pltpu.SemaphoreType.DMA((ndp,)),
        pltpu.SemaphoreType.DMA((steps, ndp)),
        pltpu.SemaphoreType.DMA((steps, ndp)),
        pltpu.SemaphoreType.DMA((steps, ntp)),
        pltpu.SemaphoreType.DMA((steps, ndp)),
        pltpu.SemaphoreType.DMA((steps, ndp, gsz)),
        pltpu.SemaphoreType.DMA((steps, ntp)),
        pltpu.SemaphoreType.DMA((steps, ntp)),
        pltpu.SemaphoreType.DMA((steps, 2)),
    ]
    vspec = pl.BlockSpec(memory_space=pltpu.VMEM)
    hspec = pl.BlockSpec(memory_space=pl.ANY)
    return pl.pallas_call(
        kernel,
        out_shape=(
            jax.ShapeDtypeStruct((steps, rows, oc), BF16),
            jax.ShapeDtypeStruct((rows, nchunk, LANES, nstate), F32),
        ),
        in_specs=[vspec] * 13 + [hspec],
        out_specs=(vspec, hspec),
        scratch_shapes=scratch,
        compiler_params=pltpu.CompilerParams(
            collective_id=0, has_side_effects=True, vmem_limit_bytes=48 * 1024 * 1024
        ),
    )


def body(
    hidden_in, pre_gain, w_zx, zx_codes, zx_exponents, w_bc, w_dt, conv_x, conv_bc, dt_bias,
    decay_rate, skip_gain, conv_state_x, conv_state_bc, ssm_state, norm_gain, w_out, out_codes,
    out_exponents,
):
    ndp, ntp = lax.axis_size("dp"), lax.axis_size("tp")
    dp = lax.axis_index("dp")
    steps, rows, feats = hidden_in.shape
    dc = feats // ndp
    lc = w_zx.shape[2]
    cb = w_bc.shape[1]
    _, heads, psize, nstate = ssm_state.shape
    gsz = ntp // G
    di = lc * ntp

    def mine(a):
        return lax.dynamic_slice_in_dim(a, dp * dc, dc, 0)

    traded = lax.all_to_all(zx_codes, "tp", split_axis=2, concat_axis=0, tiled=True)
    delta = decode_pairs(traded, zx_exponents, BLK)
    wz = (mine(w_zx).astype(F32) + delta).astype(BF16).reshape(dc, 2 * lc)
    wo = (
        lax.dynamic_slice_in_dim(w_out, dp * dc, dc, 1).astype(F32)
        + decode_matrix(out_codes, out_exponents, BLK)
    ).astype(BF16)
    ws = jnp.concatenate(
        [mine(w_bc), jnp.pad(mine(w_dt), ((0, 0), (0, LANES - heads)))], axis=1
    )
    hid = hidden_in.reshape(steps, rows, ndp, dc).transpose(2, 0, 1, 3)

    def padded(a):
        return jnp.pad(a, (0, LANES - heads))[None]

    call = make_kernel(ndp, ntp, steps, rows, dc, lc, cb, heads, psize, nstate, gsz, feats, di)
    out, state = call(
        hid, mine(pre_gain)[None], wz, ws, wo, conv_x, conv_bc, padded(dt_bias),
        padded(decay_rate), jnp.repeat(skip_gain, psize)[None], norm_gain[None],
        conv_state_x.transpose(1, 0, 2), conv_state_bc.transpose(1, 0, 2),
        ssm_state.reshape(rows, lc // LANES, LANES, nstate),
    )
    return out, state.reshape(ssm_state.shape)


def solution(mesh):
    return jax.shard_map(
        body,
        mesh=mesh,
        in_specs=(
            P(None, "dp", None),
            P(),
            P(None, None, "tp"),
            P(("dp", "tp"), None, None),
            P("dp", None, "tp"),
            P(None, "tp"),
            P(None, "tp"),
            P(None, "tp"),
            P(None, "tp"),
            P("tp"),
            P("tp"),
            P("tp"),
            P("dp", None, "tp"),
            P("dp", None, "tp"),
            P("dp", "tp", None, None),
            P("tp"),
            P("tp", None),
            P("tp", "dp"),
            P("tp", "dp"),
        ),
        out_specs=(P(None, "dp", "tp"), P("dp", "tp", None, None)),
        check_vma=False,
    )
```

```python
import jax
import jax.numpy as jnp
from jax import lax
from jax.experimental import pallas as pl
from jax.experimental.pallas import tpu as pltpu
from jax.sharding import PartitionSpec as P

G = 4
BLK = 128
LANES = 128
EPS = 1e-05
MESH = pl.DeviceIdType.MESH
F32 = jnp.float32
BF16 = jnp.bfloat16


def silu(v):
    return v / (1.0 + jnp.exp(-v))


def make_kernel(ndp, ntp, steps, rows, dc, lc, cb, heads, psize, nstate, gsz, feats, di):
    oc = feats // ntp
    ac = dc // ntp
    nchunk = lc // LANES
    hpc = LANES // psize
    small = cb + LANES
    rpd = dc // ntp

    def kernel(
        hid_ref, gain_ref, wdt_ref, sc_ref, so_ref, ocodes_ref, convx_ref, convb_ref, dtb_ref, rate_ref,
        skip_ref, ng_ref, hx0_ref, hb0_ref, state_hbm, codes_hbm, wzx_hbm, wbc_hbm, wout_hbm,
        out_ref, state_out,
        state, hx, hb, hrecv, s1, r1, s2, r2, cs, cr, gs, gr, qs, qr, os, orv, ags, agr, ms, mr,
        tbuf, rbuf, rv, wv, wz, wbc, wo,
        w_sems, v_sem, st_sem, send_sem, h_sem, sem1, sem2, c_sem, g_sem, q_sem, o_sem, a_sem, m_sem,
    ):
        dp = lax.axis_index("dp")
        tp = lax.axis_index("tp")
        pending = []

        def send(src, dst, rsem, d, t):
            copy = pltpu.make_async_remote_copy(
                src_ref=src, dst_ref=dst, send_sem=send_sem, recv_sem=rsem,
                device_id=(d, t), device_id_type=MESH,
            )
            copy.start()
            pending.append(copy)

        def recv(src, dst, rsem):
            pltpu.make_async_remote_copy(
                src_ref=src, dst_ref=dst, send_sem=send_sem, recv_sem=rsem,
                device_id=(dp, tp), device_id_type=MESH,
            ).wait_recv()

        load = pltpu.make_async_copy(state_hbm, state, st_sem)
        load_w = pltpu.make_async_copy(wzx_hbm.at[pl.ds(dp * dc, dc)], wv, w_sems.at[0])
        load_w.start()
        load_own = pltpu.make_async_copy(
            codes_hbm.at[:, :, pl.ds(pl.multiple_of(tp * lc, LANES), lc)], rv.at[tp], w_sems.at[1]
        )
        load_own.start()
        load_bc = pltpu.make_async_copy(wbc_hbm.at[pl.ds(dp * dc, dc)], wbc, w_sems.at[2])
        load_bc.start()
        load_out = pltpu.make_async_copy(
            wout_hbm.at[:, pl.ds(pl.multiple_of(dp * dc, LANES), dc)], wo, w_sems.at[3]
        )
        load_out.start()
        load.start()

        barrier = pltpu.get_barrier_semaphore()
        for i in range(ndp):
            for j in range(ntp):
                if i + j > 0:
                    pl.semaphore_signal(
                        barrier, inc=1,
                        device_id=(lax.rem(dp + i, ndp), lax.rem(tp + j, ntp)),
                        device_id_type=MESH,
                    )
        pl.semaphore_wait(barrier, ndp * ntp - 1)

        for k in range(ntp - 1, 0, -1):
            peer = tp ^ k
            send(
                codes_hbm.at[:, :, pl.ds(pl.multiple_of(peer * lc, LANES), lc)],
                rv.at[tp], v_sem.at[k], dp, peer,
            )
        for k in range(1, ndp):
            peer = lax.rem(dp + k, ndp)
            send(hid_ref.at[peer], hrecv.at[dp], h_sem.at[k], peer, tp)
        hrecv[dp] = hid_ref[dp]
        hx[0:3] = hx0_ref[...].astype(F32)
        hb[0:3] = hb0_ref[...].astype(F32)
        for k in range(1, ndp):
            src = lax.rem(dp + ndp - k, ndp)
            recv(hid_ref.at[src], hrecv.at[src], h_sem.at[k])

        load_out.wait()

        @pl.loop(0, lc // 32)
        def _(i):
            at = pl.ds(pl.multiple_of(i * 32, 32), 32)
            delta = ocodes_ref[at, :].astype(F32) * so_ref[i // (BLK // 32)]
            wo[at, :] = (wo[at, :].astype(F32) + delta).astype(BF16)

        load_w.wait()
        load_own.wait()
        load_bc.wait()
        for k in [0] + list(range(ntp - 1, 0, -1)):
            src = tp ^ k
            if k > 0:
                recv(rv.at[src], rv.at[src], v_sem.at[k])

            @pl.loop(0, rpd // 16)
            def _(i, src=src):
                first = src * rpd + i * 16
                code = rv[src, pl.ds(i * 16, 16)].astype(F32)
                old = wv[pl.ds(first, 16)].astype(F32)
                new = old + code * sc_ref[src * rpd // BLK][None]
                wz[pl.ds(pl.multiple_of(2 * first, 32), 32), :] = new.astype(BF16).reshape(32, lc)

        lane = lax.broadcasted_iota(jnp.int32, (rows, LANES), 1)
        lane_all = lax.broadcasted_iota(jnp.int32, (ndp * rows, LANES), 1)
        lane_sq = lax.broadcasted_iota(jnp.int32, (LANES, LANES), 1)
        put_row = lax.broadcasted_iota(jnp.int32, (LANES, 2 * LANES), 0)
        put_col = lax.broadcasted_iota(jnp.int32, (LANES, 2 * LANES), 1)
        owner = tp * oc // dc
        half = (tp * oc - owner * dc) // oc
        group = tp // gsz
        member = tp - group * gsz
        carried = None
        for s in range(steps):
            x = jnp.concatenate([hrecv[d, s].astype(F32) for d in range(ndp)], axis=0)
            if s > 0:
                x = x + carried
            ss = jnp.sum(x * x, axis=1, keepdims=True)
            y = (x * gain_ref[...]).astype(BF16)
            p = jnp.dot(y, wbc[...], preferred_element_type=F32)
            last = jnp.dot(y, wdt_ref[...], preferred_element_type=F32)
            last = jnp.where(lane_all == LANES - 1, ss, last)
            for d in range(ndp):
                at = slice(d * rows, (d + 1) * rows)
                s1[s, d, :, :cb] = p[at]
                s1[s, d, :, cb:] = last[at]
            for k in range(1, ndp):
                peer = lax.rem(dp + k, ndp)
                send(s1.at[s, peer], r1.at[s, k], sem1.at[s, k], peer, tp)
            spread = []
            for half_of in range(2):
                place = (put_col == 2 * put_row + half_of).astype(BF16)
                parts = [
                    jnp.dot(y[:, c : c + LANES], place, preferred_element_type=F32).astype(BF16)
                    for c in range(0, dc, LANES)
                ]
                spread.append(jnp.concatenate(parts, axis=1))
            spread = jnp.concatenate(spread, axis=0)
            width = min(256, lc)
            for c in range(0, lc, width):
                p = jnp.dot(spread, wz[:, c : c + width], preferred_element_type=F32)
                for d in range(ndp):
                    s2[s, d, :, c : c + width] = p[d * rows : (d + 1) * rows]
                    s2[s, d, :, lc + c : lc + c + width] = p[
                        (ndp + d) * rows : (ndp + d + 1) * rows
                    ]
            for k in range(1, ndp):
                peer = lax.rem(dp + k, ndp)
                send(s2.at[s, peer], r2.at[s, k], sem2.at[s, k], peer, tp)
            for k in range(1, ndp):
                recv(s1.at[s, 0], r1.at[s, k], sem1.at[s, k])
            total = s1[s, dp]
            for k in range(1, ndp):
                total = total + r1[s, k]
            inv = lax.rsqrt(total[:, small - 1 :] / feats + EPS)
            hb[s + 3] = total[:, :cb] * inv
            mixed = convb_ref[4:5, :]
            for i in range(4):
                mixed = mixed + hb[s + i] * convb_ref[i : i + 1, :]
            piece = silu(mixed)
            cs[s] = piece
            cr[s, tp] = piece
            for k in range(1, ntp):
                send(cs.at[s], cr.at[s, tp], c_sem.at[s, k], dp, lax.rem(tp + k, ntp))
            z = total[:, cb:] * inv + dtb_ref[...]
            dt = jnp.maximum(z, 0.0) + jnp.log1p(jnp.exp(-jnp.abs(z)))
            decay = jnp.exp(-dt * rate_ref[...])

            for k in range(1, ndp):
                recv(s2.at[s, 0], r2.at[s, k], sem2.at[s, k])
            inners = []
            for j in range(nchunk):
                at = slice(lc + j * LANES, lc + (j + 1) * LANES)
                here = slice(j * LANES, (j + 1) * LANES)
                v = s2[s, dp, :, at]
                for k in range(1, ndp):
                    v = v + r2[s, k, :, at]
                hx[s + 3, :, here] = v * inv
                mixed = convx_ref[4:5, here]
                for i in range(4):
                    mixed = mixed + hx[s + i, :, here] * convx_ref[i : i + 1, here]
                inner = silu(mixed)
                inners.append(inner)
                dte = jnp.zeros((rows, LANES), F32)
                dece = jnp.zeros((rows, LANES), F32)
                for i in range(hpc):
                    h = j * hpc + i
                    inside = (lane >= i * psize) & (lane < (i + 1) * psize)
                    dte = jnp.where(inside, dt[:, h : h + 1], dte)
                    dece = jnp.where(inside, decay[:, h : h + 1], dece)
                tbuf[j, :rows] = dte * inner
                tbuf[j, rows:] = dece
            for k in range(1, ntp):
                src = lax.rem(tp + ntp - k, ntp)
                recv(cs.at[s], cr.at[s, src], c_sem.at[s, k])
            per = nstate // cb
            b0 = group * nstate // cb
            bmat = [cr[s, b0 + i] for i in range(per)]
            cmat = [cr[s, G * nstate // cb + b0 + i] for i in range(per)]
            bmat = bmat[0] if per == 1 else jnp.concatenate(bmat, axis=1)
            cmat = cmat[0] if per == 1 else jnp.concatenate(cmat, axis=1)
            if s == 0:
                load.wait()

            @pl.loop(0, nchunk)
            def _(j):
                full = jnp.concatenate(
                    [tbuf[j], jnp.zeros((LANES - 2 * rows, LANES), F32)], axis=0
                )
                flipped = full.T
                acc = jnp.zeros((LANES, LANES), F32)
                for r in range(rows):
                    new = (
                        flipped[:, rows + r : rows + r + 1] * state[r, j]
                        + flipped[:, r : r + 1] * bmat[r : r + 1, :]
                    )
                    state[r, j] = new
                    q = jnp.sum(new * cmat[r : r + 1, :], axis=1, keepdims=True)
                    acc = jnp.where(lane_sq == r, q, acc)
                rbuf[j] = acc.T[:rows]

            if s == steps - 1:
                store = pltpu.make_async_copy(state, state_out, st_sem)
                store.start()
            ss = jnp.zeros((rows, LANES), F32)
            for j in range(nchunk):
                here = slice(j * LANES, (j + 1) * LANES)
                v = s2[s, dp, :, here]
                for k in range(1, ndp):
                    v = v + r2[s, k, :, here]
                gated = (rbuf[j] + skip_ref[:, here] * inners[j]) * silu(v * inv)
                ss = ss + gated * gated
                gs[s, :, here] = (gated * ng_ref[:, here]).astype(BF16)
            qs[s] = jnp.broadcast_to(jnp.sum(ss, axis=1, keepdims=True), (rows, LANES))
            gr[s, dp] = gs[s]
            qr[s, dp, member] = qs[s]
            for k in range(1, ndp):
                send(gs.at[s], gr.at[s, dp], g_sem.at[s, k], lax.rem(dp + k, ndp), tp)
            for k in range(ndp):
                for m in range(gsz):
                    if k + m > 0:
                        send(
                            qs.at[s], qr.at[s, dp, member], q_sem.at[s, k, m],
                            lax.rem(dp + k, ndp), group * gsz + lax.rem(member + m, gsz),
                        )
            for k in range(ndp):
                src = lax.rem(dp + ndp - k, ndp)
                if k > 0:
                    recv(gs.at[s], gr.at[s, src], g_sem.at[s, k])
                for m in range(gsz):
                    if k + m > 0:
                        frm = lax.rem(member + gsz - m, gsz)
                        recv(qs.at[s], qr.at[s, src, frm], q_sem.at[s, k, m])
            every = jnp.concatenate(
                [gr[s, d].astype(F32) for d in range(ndp)], axis=0
            ).astype(BF16)
            scales = []
            for d in range(ndp):
                sq = qr[s, d, 0]
                for m in range(1, gsz):
                    sq = sq + qr[s, d, m]
                scales.append(lax.rsqrt(sq[:, :1] / (di // G) + EPS))
            scale = jnp.concatenate(scales, axis=0)
            width = max(ac, min(256, dc))
            for c in range(0, dc, width):
                p = jnp.dot(every, wo[:, c : c + width], preferred_element_type=F32) * scale
                for i in range(width // ac):
                    os[s, c // ac + i] = p[:, i * ac : (i + 1) * ac]
            for k in range(1, ntp):
                peer = lax.rem(tp + k, ntp)
                send(os.at[s, peer], orv.at[s, k], o_sem.at[s, k], dp, peer)
            for k in range(1, ntp):
                recv(os.at[s, 0], orv.at[s, k], o_sem.at[s, k])
            total = os[s, tp]
            for k in range(1, ntp):
                total = total + orv[s, k]
            total = total.astype(BF16)
            ags[s] = total
            agr[s, tp] = total
            for k in range(1, ntp):
                send(ags.at[s], agr.at[s, tp], a_sem.at[s, k], dp, lax.rem(tp + k, ntp))
            for k in range(1, ntp):
                src = lax.rem(tp + ntp - k, ntp)
                recv(ags.at[s], agr.at[s, src], a_sem.at[s, k])
            carried = jnp.concatenate([agr[s, t].astype(F32) for t in range(ntp)], axis=1)
            picked = carried[:, :oc]
            for i in range(1, dc // oc):
                picked = jnp.where(half == i, carried[:, i * oc : (i + 1) * oc], picked)
            for d in range(ndp):
                ms[s, d] = picked[d * rows : (d + 1) * rows].astype(BF16)

            @pl.when(owner == dp)
            def _():
                for k in range(1, ndp):
                    peer = lax.rem(dp + k, ndp)
                    pltpu.make_async_remote_copy(
                        src_ref=ms.at[s, peer], dst_ref=mr.at[s], send_sem=m_sem.at[s, 0],
                        recv_sem=m_sem.at[s, 1], device_id=(peer, tp), device_id_type=MESH,
                    ).start()

        store.wait()
        for s in range(steps):
            def final(s=s):
                return pltpu.make_async_remote_copy(
                    src_ref=ms.at[s, 0], dst_ref=mr.at[s], send_sem=m_sem.at[s, 0],
                    recv_sem=m_sem.at[s, 1], device_id=(dp, tp), device_id_type=MESH,
                )

            @pl.when(owner == dp)
            def _():
                out_ref[s] = ms[s, dp]
                for k in range(1, ndp):
                    final().wait_send()

            @pl.when(owner != dp)
            def _():
                final().wait_recv()
                out_ref[s] = mr[s]

        for copy in pending:
            copy.wait_send()

    vm = pltpu.VMEM
    scratch = [
        vm((rows, nchunk, LANES, nstate), F32),
        vm((steps + 3, rows, lc), F32),
        vm((steps + 3, rows, cb), F32),
        vm((ndp, steps, rows, dc), BF16),
        vm((steps, ndp, rows, small), F32),
        vm((steps, ndp, rows, small), F32),
        vm((steps, ndp, rows, 2 * lc), F32),
        vm((steps, ndp, rows, 2 * lc), F32),
        vm((steps, rows, cb), F32),
        vm((steps, ntp, rows, cb), F32),
        vm((steps, rows, lc), BF16),
        vm((steps, ndp, rows, lc), BF16),
        vm((steps, rows, LANES), F32),
        vm((steps, ndp, gsz, rows, LANES), F32),
        vm((steps, ntp, ndp * rows, ac), F32),
        vm((steps, ntp, ndp * rows, ac), F32),
        vm((steps, ndp * rows, ac), BF16),
        vm((steps, ntp, ndp * rows, ac), BF16),
        vm((steps, ndp, rows, oc), BF16),
        vm((steps, rows, oc), BF16),
        vm((nchunk, 2 * rows, LANES), F32),
        vm((nchunk, rows, LANES), F32),
        vm((ntp, rpd, 2, lc), BF16),
        vm((dc, 2, lc), BF16),
        vm((2 * dc, lc), BF16),
        vm((dc, cb), BF16),
        vm((lc, dc), BF16),
        pltpu.SemaphoreType.DMA((4,)),
        pltpu.SemaphoreType.DMA((ntp,)),
        pltpu.SemaphoreType.DMA(()),
        pltpu.SemaphoreType.DMA(()),
        pltpu.SemaphoreType.DMA((ndp,)),
        pltpu.SemaphoreType.DMA((steps, ndp)),
        pltpu.SemaphoreType.DMA((steps, ndp)),
        pltpu.SemaphoreType.DMA((steps, ntp)),
        pltpu.SemaphoreType.DMA((steps, ndp)),
        pltpu.SemaphoreType.DMA((steps, ndp, gsz)),
        pltpu.SemaphoreType.DMA((steps, ntp)),
        pltpu.SemaphoreType.DMA((steps, ntp)),
        pltpu.SemaphoreType.DMA((steps, 2)),
    ]
    vspec = pl.BlockSpec(memory_space=pltpu.VMEM)
    hspec = pl.BlockSpec(memory_space=pl.ANY)
    return pl.pallas_call(
        kernel,
        out_shape=(
            jax.ShapeDtypeStruct((steps, rows, oc), BF16),
            jax.ShapeDtypeStruct((rows, nchunk, LANES, nstate), F32),
        ),
        in_specs=[vspec] * 14 + [hspec] * 5,
        out_specs=(vspec, hspec),
        scratch_shapes=scratch,
        compiler_params=pltpu.CompilerParams(
            collective_id=0, has_side_effects=True, vmem_limit_bytes=48 * 1024 * 1024
        ),
    )


def body(
    hidden_in, pre_gain, w_zx, zx_codes, zx_exponents, w_bc, w_dt, conv_x, conv_bc, dt_bias,
    decay_rate, skip_gain, conv_state_x, conv_state_bc, ssm_state, norm_gain, w_out, out_codes,
    out_exponents,
):
    ndp, ntp = lax.axis_size("dp"), lax.axis_size("tp")
    dp = lax.axis_index("dp")
    steps, rows, feats = hidden_in.shape
    dc = feats // ndp
    lc = w_zx.shape[2]
    cb = w_bc.shape[1]
    _, heads, psize, nstate = ssm_state.shape
    gsz = ntp // G
    di = lc * ntp

    def mine(a):
        return lax.dynamic_slice_in_dim(a, dp * dc, dc, 0)

    sc = jnp.repeat(jnp.exp2(zx_exponents.astype(F32)), BLK, axis=2)
    so = jnp.repeat(jnp.exp2(out_exponents.astype(F32)), BLK, axis=1)[:, None]
    wdt = jnp.pad(mine(w_dt), ((0, 0), (0, LANES - heads)))
    hid = hidden_in.reshape(steps, rows, ndp, dc).transpose(2, 0, 1, 3)

    def padded(a):
        return jnp.pad(a, (0, LANES - heads))[None]

    call = make_kernel(ndp, ntp, steps, rows, dc, lc, cb, heads, psize, nstate, gsz, feats, di)
    out, state = call(
        hid, mine(pre_gain)[None], wdt, sc, so, out_codes, conv_x, conv_bc, padded(dt_bias),
        padded(decay_rate), jnp.repeat(skip_gain, psize)[None], norm_gain[None],
        conv_state_x.transpose(1, 0, 2), conv_state_bc.transpose(1, 0, 2),
        ssm_state.reshape(rows, lc // LANES, LANES, nstate),
        zx_codes, w_zx, w_bc, w_out,
    )
    return out, state.reshape(ssm_state.shape)


def solution(mesh):
    return jax.shard_map(
        body,
        mesh=mesh,
        in_specs=(
            P(None, "dp", None),
            P(),
            P(None, None, "tp"),
            P(("dp", "tp"), None, None),
            P("dp", None, "tp"),
            P(None, "tp"),
            P(None, "tp"),
            P(None, "tp"),
            P(None, "tp"),
            P("tp"),
            P("tp"),
            P("tp"),
            P("dp", None, "tp"),
            P("dp", None, "tp"),
            P("dp", "tp", None, None),
            P("tp"),
            P("tp", None),
            P("tp", "dp"),
            P("tp", "dp"),
        ),
        out_specs=(P(None, "dp", "tp"), P("dp", "tp", None, None)),
        check_vma=False,
    )
```

```python
import jax
import jax.numpy as jnp
from jax import lax
from jax.experimental import pallas as pl
from jax.experimental.pallas import tpu as pltpu
from jax.sharding import PartitionSpec as P

G = 4
BLK = 128
LANES = 128
EPS = 1e-05
MESH = pl.DeviceIdType.MESH
F32 = jnp.float32
BF16 = jnp.bfloat16


def silu(v):
    return v / (1.0 + jnp.exp(-v))


def make_kernel(ndp, ntp, steps, rows, dc, lc, cb, heads, psize, nstate, gsz, feats, di):
    oc = feats // ntp
    ac = dc // ntp
    nchunk = lc // LANES
    hpc = LANES // psize
    small = cb + LANES
    rpd = dc // ntp

    def kernel(
        hid_hbm, gain_hbm, wdt_hbm, sc_hbm, so_hbm, ocodes_hbm, convx_hbm, convb_hbm, dtb_hbm,
        rate_hbm, skip_hbm, ng_hbm, hx0_hbm, hb0_hbm, state_hbm, codes_hbm, wzx_hbm, wbc_hbm,
        wout_hbm,
        out_ref, state_out,
        state, hx, hb, hrecv, s1, r1, s2, r2, cs, cr, gs, gr, qs, qr, os, orv, ags, agr, ms, mr,
        tbuf, rbuf, rv, wv, wz, wbc, wo,
        gain_ref, wdt_in, wdt_ref, sc_in, sc_ref, so_in, so_ref, ocodes_ref, convx_ref, convb_ref,
        dtb_ref, rate_ref, skip_ref, ng_ref, hx0_ref, hb0_ref, l_sems,
        w_sems, v_sem, st_sem, send_sem, h_sem, sem1, sem2, c_sem, g_sem, q_sem, o_sem, a_sem, m_sem,
    ):
        dp = lax.axis_index("dp")
        tp = lax.axis_index("tp")
        pending = []

        def send(src, dst, rsem, d, t):
            copy = pltpu.make_async_remote_copy(
                src_ref=src, dst_ref=dst, send_sem=send_sem, recv_sem=rsem,
                device_id=(d, t), device_id_type=MESH,
            )
            copy.start()
            pending.append(copy)

        def recv(src, dst, rsem):
            pltpu.make_async_remote_copy(
                src_ref=src, dst_ref=dst, send_sem=send_sem, recv_sem=rsem,
                device_id=(dp, tp), device_id_type=MESH,
            ).wait_recv()

        load = pltpu.make_async_copy(state_hbm, state, st_sem)
        load_w = pltpu.make_async_copy(wzx_hbm.at[pl.ds(dp * dc, dc)], wv, w_sems.at[0])
        load_w.start()
        load_own = pltpu.make_async_copy(
            codes_hbm.at[:, :, pl.ds(pl.multiple_of(tp * lc, LANES), lc)], rv.at[tp], w_sems.at[1]
        )
        load_own.start()
        load_bc = pltpu.make_async_copy(wbc_hbm.at[pl.ds(dp * dc, dc)], wbc, w_sems.at[2])
        load_bc.start()
        load_out = pltpu.make_async_copy(
            wout_hbm.at[:, pl.ds(pl.multiple_of(dp * dc, LANES), dc)], wo, w_sems.at[3]
        )
        load_out.start()
        load.start()

        def chunk(i):
            return pl.ds(pl.multiple_of(i * dc, LANES), dc)

        small_loads = [
            (gain_hbm.at[:, chunk(dp)], gain_ref), (wdt_hbm.at[:, chunk(dp)], wdt_in),
            (sc_hbm, sc_in), (so_hbm, so_in), (ocodes_hbm, ocodes_ref), (convx_hbm, convx_ref),
            (convb_hbm, convb_ref), (dtb_hbm, dtb_ref), (rate_hbm, rate_ref),
            (skip_hbm, skip_ref), (ng_hbm, ng_ref), (hx0_hbm, hx0_ref), (hb0_hbm, hb0_ref),
            (hid_hbm.at[:, :, chunk(dp)], hrecv.at[dp]),
        ]
        small_loads = [
            pltpu.make_async_copy(a, b, l_sems.at[i]) for i, (a, b) in enumerate(small_loads)
        ]
        for copy in small_loads:
            copy.start()

        barrier = pltpu.get_barrier_semaphore()
        for i in range(ndp):
            for j in range(ntp):
                if i + j > 0:
                    pl.semaphore_signal(
                        barrier, inc=1,
                        device_id=(lax.rem(dp + i, ndp), lax.rem(tp + j, ntp)),
                        device_id_type=MESH,
                    )
        pl.semaphore_wait(barrier, ndp * ntp - 1)

        for k in range(ntp - 1, 0, -1):
            peer = tp ^ k
            send(
                codes_hbm.at[:, :, pl.ds(pl.multiple_of(peer * lc, LANES), lc)],
                rv.at[tp], v_sem.at[k], dp, peer,
            )
        for k in range(1, ndp):
            peer = lax.rem(dp + k, ndp)
            send(hid_hbm.at[:, :, chunk(peer)], hrecv.at[dp], h_sem.at[k], peer, tp)
        for copy in small_loads:
            copy.wait()
        wdt_ref[...] = jnp.concatenate(
            [wdt_in[...].astype(F32), jnp.zeros((LANES - heads, dc), F32)], axis=0
        ).astype(BF16)
        for ref, table in ((sc_in, sc_ref), (so_in, so_ref)):
            power = jnp.exp2(ref[...].astype(F32))
            nrow, pair, ncol = power.shape
            for b in range(nrow):
                table[b] = jnp.concatenate(
                    [
                        jnp.broadcast_to(power[b, :, c : c + 1], (pair, BLK))
                        for c in range(ncol)
                    ],
                    axis=1,
                )
        hx[0:3] = hx0_ref[...].astype(F32)
        hb[0:3] = hb0_ref[...].astype(F32)
        for k in range(1, ndp):
            src = lax.rem(dp + ndp - k, ndp)
            recv(hrecv.at[src], hrecv.at[src], h_sem.at[k])

        load_out.wait()

        @pl.loop(0, lc // 32)
        def _(i):
            at = pl.ds(pl.multiple_of(i * 32, 32), 32)
            delta = ocodes_ref[at, :].astype(F32) * so_ref[i // (BLK // 32)]
            wo[at, :] = (wo[at, :].astype(F32) + delta).astype(BF16)

        load_w.wait()
        load_own.wait()
        load_bc.wait()
        for k in [0] + list(range(ntp - 1, 0, -1)):
            src = tp ^ k
            if k > 0:
                recv(rv.at[src], rv.at[src], v_sem.at[k])

            @pl.loop(0, rpd // 16)
            def _(i, src=src):
                first = src * rpd + i * 16
                code = rv[src, pl.ds(i * 16, 16)].astype(F32)
                old = wv[pl.ds(first, 16)].astype(F32)
                new = old + code * sc_ref[src * rpd // BLK][None]
                wz[pl.ds(pl.multiple_of(2 * first, 32), 32), :] = new.astype(BF16).reshape(32, lc)

        lane = lax.broadcasted_iota(jnp.int32, (rows, LANES), 1)
        lane_all = lax.broadcasted_iota(jnp.int32, (ndp * rows, LANES), 1)
        lane_sq = lax.broadcasted_iota(jnp.int32, (LANES, LANES), 1)
        put_row = lax.broadcasted_iota(jnp.int32, (LANES, 2 * LANES), 0)
        put_col = lax.broadcasted_iota(jnp.int32, (LANES, 2 * LANES), 1)
        owner = tp * oc // dc
        half = (tp * oc - owner * dc) // oc
        group = tp // gsz
        member = tp - group * gsz
        carried = None
        for s in range(steps):
            x = jnp.concatenate([hrecv[d, s].astype(F32) for d in range(ndp)], axis=0)
            if s > 0:
                x = x + carried
            ss = jnp.sum(x * x, axis=1, keepdims=True)
            y = (x * gain_ref[...]).astype(BF16)
            p = jnp.dot(y, wbc[...], preferred_element_type=F32)
            last = lax.dot_general(
                y, wdt_ref[...], (((1,), (1,)), ((), ())), preferred_element_type=F32
            )
            last = jnp.where(lane_all == LANES - 1, ss, last)
            for d in range(ndp):
                at = slice(d * rows, (d + 1) * rows)
                s1[s, d, :, :cb] = p[at]
                s1[s, d, :, cb:] = last[at]
            for k in range(1, ndp):
                peer = lax.rem(dp + k, ndp)
                send(s1.at[s, peer], r1.at[s, k], sem1.at[s, k], peer, tp)
            spread = []
            for half_of in range(2):
                place = (put_col == 2 * put_row + half_of).astype(BF16)
                parts = [
                    jnp.dot(y[:, c : c + LANES], place, preferred_element_type=F32).astype(BF16)
                    for c in range(0, dc, LANES)
                ]
                spread.append(jnp.concatenate(parts, axis=1))
            spread = jnp.concatenate(spread, axis=0)
            width = min(256, lc)
            for c in range(0, lc, width):
                p = jnp.dot(spread, wz[:, c : c + width], preferred_element_type=F32)
                for d in range(ndp):
                    s2[s, d, :, c : c + width] = p[d * rows : (d + 1) * rows].astype(BF16)
                    s2[s, d, :, lc + c : lc + c + width] = p[
                        (ndp + d) * rows : (ndp + d + 1) * rows
                    ].astype(BF16)
            for k in range(1, ndp):
                peer = lax.rem(dp + k, ndp)
                send(s2.at[s, peer], r2.at[s, k], sem2.at[s, k], peer, tp)
            for k in range(1, ndp):
                recv(s1.at[s, 0], r1.at[s, k], sem1.at[s, k])
            total = s1[s, dp]
            for k in range(1, ndp):
                total = total + r1[s, k]
            inv = lax.rsqrt(total[:, small - 1 :] / feats + EPS)
            hb[s + 3] = total[:, :cb] * inv
            mixed = convb_ref[4:5, :]
            for i in range(4):
                mixed = mixed + hb[s + i] * convb_ref[i : i + 1, :]
            piece = silu(mixed)
            cs[s] = piece
            cr[s, tp] = piece
            for k in range(1, ntp):
                send(cs.at[s], cr.at[s, tp], c_sem.at[s, k], dp, lax.rem(tp + k, ntp))
            z = total[:, cb : cb + heads] * inv + dtb_ref[...]
            dt = jnp.maximum(z, 0.0) + jnp.log1p(jnp.exp(-jnp.abs(z)))
            decay = jnp.exp(-dt * rate_ref[...])

            for k in range(1, ndp):
                recv(s2.at[s, 0], r2.at[s, k], sem2.at[s, k])
            inners = []
            for j in range(nchunk):
                at = slice(lc + j * LANES, lc + (j + 1) * LANES)
                here = slice(j * LANES, (j + 1) * LANES)
                v = s2[s, dp, :, at].astype(F32)
                for k in range(1, ndp):
                    v = v + r2[s, k, :, at].astype(F32)
                hx[s + 3, :, here] = v * inv
                mixed = convx_ref[4:5, here]
                for i in range(4):
                    mixed = mixed + hx[s + i, :, here] * convx_ref[i : i + 1, here]
                inner = silu(mixed)
                dte = jnp.zeros((rows, LANES), F32)
                dece = jnp.zeros((rows, LANES), F32)
                skip = jnp.zeros((rows, LANES), F32)
                for i in range(hpc):
                    h = j * hpc + i
                    inside = (lane >= i * psize) & (lane < (i + 1) * psize)
                    dte = jnp.where(inside, dt[:, h : h + 1], dte)
                    dece = jnp.where(inside, decay[:, h : h + 1], dece)
                    skip = jnp.where(inside, skip_ref[:, h : h + 1], skip)
                inners.append(skip * inner)
                tbuf[j, :rows] = dte * inner
                tbuf[j, rows:] = dece
            for k in range(1, ntp):
                src = lax.rem(tp + ntp - k, ntp)
                recv(cs.at[s], cr.at[s, src], c_sem.at[s, k])
            per = nstate // cb
            b0 = group * nstate // cb
            bmat = [cr[s, b0 + i] for i in range(per)]
            cmat = [cr[s, G * nstate // cb + b0 + i] for i in range(per)]
            bmat = bmat[0] if per == 1 else jnp.concatenate(bmat, axis=1)
            cmat = cmat[0] if per == 1 else jnp.concatenate(cmat, axis=1)
            if s == 0:
                load.wait()

            @pl.loop(0, nchunk)
            def _(j):
                full = jnp.concatenate(
                    [tbuf[j], jnp.zeros((LANES - 2 * rows, LANES), F32)], axis=0
                )
                flipped = full.T
                acc = jnp.zeros((LANES, LANES), F32)
                for r in range(rows):
                    new = (
                        flipped[:, rows + r : rows + r + 1] * state[r, j]
                        + flipped[:, r : r + 1] * bmat[r : r + 1, :]
                    )
                    state[r, j] = new
                    q = jnp.sum(new * cmat[r : r + 1, :], axis=1, keepdims=True)
                    acc = jnp.where(lane_sq == r, q, acc)
                rbuf[j] = acc.T[:rows]

            if s == steps - 1:
                store = pltpu.make_async_copy(state, state_out, st_sem)
                store.start()
            ss = jnp.zeros((rows, LANES), F32)
            for j in range(nchunk):
                here = slice(j * LANES, (j + 1) * LANES)
                v = s2[s, dp, :, here].astype(F32)
                for k in range(1, ndp):
                    v = v + r2[s, k, :, here].astype(F32)
                gated = (rbuf[j] + inners[j]) * silu(v * inv)
                ss = ss + gated * gated
                gs[s, :, here] = (gated * ng_ref[:, here]).astype(BF16)
            qs[s] = jnp.broadcast_to(jnp.sum(ss, axis=1, keepdims=True), (rows, LANES))
            gr[s, dp] = gs[s]
            qr[s, dp, member] = qs[s]
            for k in range(1, ndp):
                send(gs.at[s], gr.at[s, dp], g_sem.at[s, k], lax.rem(dp + k, ndp), tp)
            for k in range(ndp):
                for m in range(gsz):
                    if k + m > 0:
                        send(
                            qs.at[s], qr.at[s, dp, member], q_sem.at[s, k, m],
                            lax.rem(dp + k, ndp), group * gsz + lax.rem(member + m, gsz),
                        )
            for k in range(ndp):
                src = lax.rem(dp + ndp - k, ndp)
                if k > 0:
                    recv(gs.at[s], gr.at[s, src], g_sem.at[s, k])
                for m in range(gsz):
                    if k + m > 0:
                        frm = lax.rem(member + gsz - m, gsz)
                        recv(qs.at[s], qr.at[s, src, frm], q_sem.at[s, k, m])
            every = jnp.concatenate(
                [gr[s, d].astype(F32) for d in range(ndp)], axis=0
            ).astype(BF16)
            scales = []
            for d in range(ndp):
                sq = qr[s, d, 0]
                for m in range(1, gsz):
                    sq = sq + qr[s, d, m]
                scales.append(lax.rsqrt(sq[:, :1] / (di // G) + EPS))
            scale = jnp.concatenate(scales, axis=0)
            width = max(ac, min(256, dc))
            for c in range(0, dc, width):
                p = jnp.dot(every, wo[:, c : c + width], preferred_element_type=F32) * scale
                for i in range(width // ac):
                    os[s, c // ac + i] = p[:, i * ac : (i + 1) * ac].astype(BF16)
            for k in range(1, ntp):
                peer = lax.rem(tp + k, ntp)
                send(os.at[s, peer], orv.at[s, k], o_sem.at[s, k], dp, peer)
            for k in range(1, ntp):
                recv(os.at[s, 0], orv.at[s, k], o_sem.at[s, k])
            total = os[s, tp].astype(F32)
            for k in range(1, ntp):
                total = total + orv[s, k].astype(F32)
            total = total.astype(BF16)
            ags[s] = total
            agr[s, tp] = total
            for k in range(1, ntp):
                send(ags.at[s], agr.at[s, tp], a_sem.at[s, k], dp, lax.rem(tp + k, ntp))
            for k in range(1, ntp):
                src = lax.rem(tp + ntp - k, ntp)
                recv(ags.at[s], agr.at[s, src], a_sem.at[s, k])
            carried = jnp.concatenate([agr[s, t].astype(F32) for t in range(ntp)], axis=1)
            picked = carried[:, :oc]
            for i in range(1, dc // oc):
                picked = jnp.where(half == i, carried[:, i * oc : (i + 1) * oc], picked)
            for d in range(ndp):
                ms[s, d] = picked[d * rows : (d + 1) * rows].astype(BF16)

            @pl.when(owner == dp)
            def _():
                for k in range(1, ndp):
                    peer = lax.rem(dp + k, ndp)
                    pltpu.make_async_remote_copy(
                        src_ref=ms.at[s, peer], dst_ref=mr.at[s], send_sem=m_sem.at[s, 0],
                        recv_sem=m_sem.at[s, 1], device_id=(peer, tp), device_id_type=MESH,
                    ).start()

        store.wait()
        for s in range(steps):
            def final(s=s):
                return pltpu.make_async_remote_copy(
                    src_ref=ms.at[s, 0], dst_ref=mr.at[s], send_sem=m_sem.at[s, 0],
                    recv_sem=m_sem.at[s, 1], device_id=(dp, tp), device_id_type=MESH,
                )

            @pl.when(owner == dp)
            def _():
                out_ref[s] = ms[s, dp]
                for k in range(1, ndp):
                    final().wait_send()

            @pl.when(owner != dp)
            def _():
                final().wait_recv()
                out_ref[s] = mr[s]

        for copy in pending:
            copy.wait_send()

    vm = pltpu.VMEM
    scratch = [
        vm((rows, nchunk, LANES, nstate), F32),
        vm((steps + 3, rows, lc), F32),
        vm((steps + 3, rows, cb), F32),
        vm((ndp, steps, rows, dc), BF16),
        vm((steps, ndp, rows, small), F32),
        vm((steps, ndp, rows, small), F32),
        vm((steps, ndp, rows, 2 * lc), BF16),
        vm((steps, ndp, rows, 2 * lc), BF16),
        vm((steps, rows, cb), F32),
        vm((steps, ntp, rows, cb), F32),
        vm((steps, rows, lc), BF16),
        vm((steps, ndp, rows, lc), BF16),
        vm((steps, rows, LANES), F32),
        vm((steps, ndp, gsz, rows, LANES), F32),
        vm((steps, ntp, ndp * rows, ac), BF16),
        vm((steps, ntp, ndp * rows, ac), BF16),
        vm((steps, ndp * rows, ac), BF16),
        vm((steps, ntp, ndp * rows, ac), BF16),
        vm((steps, ndp, rows, oc), BF16),
        vm((steps, rows, oc), BF16),
        vm((nchunk, 2 * rows, LANES), F32),
        vm((nchunk, rows, LANES), F32),
        vm((ntp, rpd, 2, lc), BF16),
        vm((dc, 2, lc), BF16),
        vm((2 * dc, lc), BF16),
        vm((dc, cb), BF16),
        vm((lc, dc), BF16),
        vm((1, dc), F32),
        vm((heads, dc), BF16),
        vm((LANES, dc), BF16),
        vm((dc // BLK, 2, lc // BLK), jnp.int32),
        vm((dc // BLK, 2, lc), F32),
        vm((lc // BLK, 1, dc // BLK), jnp.int32),
        vm((lc // BLK, 1, dc), F32),
        vm((lc, dc), BF16),
        vm((5, lc), F32),
        vm((5, cb), F32),
        vm((1, heads), F32),
        vm((1, heads), F32),
        vm((1, heads), F32),
        vm((1, lc), F32),
        vm((3, rows, lc), BF16),
        vm((3, rows, cb), BF16),
        pltpu.SemaphoreType.DMA((14,)),
        pltpu.SemaphoreType.DMA((4,)),
        pltpu.SemaphoreType.DMA((ntp,)),
        pltpu.SemaphoreType.DMA(()),
        pltpu.SemaphoreType.DMA(()),
        pltpu.SemaphoreType.DMA((ndp,)),
        pltpu.SemaphoreType.DMA((steps, ndp)),
        pltpu.SemaphoreType.DMA((steps, ndp)),
        pltpu.SemaphoreType.DMA((steps, ntp)),
        pltpu.SemaphoreType.DMA((steps, ndp)),
        pltpu.SemaphoreType.DMA((steps, ndp, gsz)),
        pltpu.SemaphoreType.DMA((steps, ntp)),
        pltpu.SemaphoreType.DMA((steps, ntp)),
        pltpu.SemaphoreType.DMA((steps, 2)),
    ]
    vspec = pl.BlockSpec(memory_space=pltpu.VMEM)
    hspec = pl.BlockSpec(memory_space=pl.ANY)
    return pl.pallas_call(
        kernel,
        out_shape=(
            jax.ShapeDtypeStruct((steps, rows, oc), BF16),
            jax.ShapeDtypeStruct((rows, nchunk, LANES, nstate), F32),
        ),
        in_specs=[hspec] * 19,
        out_specs=(vspec, hspec),
        scratch_shapes=scratch,
        compiler_params=pltpu.CompilerParams(
            collective_id=0, has_side_effects=True, vmem_limit_bytes=60 * 1024 * 1024
        ),
    )


def body(
    hidden_in, pre_gain, w_zx, zx_codes, zx_exponents, w_bc, w_dt, conv_x, conv_bc, dt_bias,
    decay_rate, skip_gain, conv_state_x, conv_state_bc, ssm_state, norm_gain, w_out, out_codes,
    out_exponents,
):
    ndp, ntp = lax.axis_size("dp"), lax.axis_size("tp")
    steps, rows, feats = hidden_in.shape
    dc = feats // ndp
    lc = w_zx.shape[2]
    cb = w_bc.shape[1]
    _, heads, psize, nstate = ssm_state.shape
    gsz = ntp // G
    di = lc * ntp

    call = make_kernel(ndp, ntp, steps, rows, dc, lc, cb, heads, psize, nstate, gsz, feats, di)
    out, state = call(
        hidden_in, pre_gain[None], w_dt.T, zx_exponents, out_exponents[:, None], out_codes, conv_x,
        conv_bc, dt_bias[None], decay_rate[None], skip_gain[None], norm_gain[None],
        conv_state_x.transpose(1, 0, 2), conv_state_bc.transpose(1, 0, 2),
        ssm_state.reshape(rows, lc // LANES, LANES, nstate),
        zx_codes, w_zx, w_bc, w_out,
    )
    return out, state.reshape(ssm_state.shape)


def solution(mesh):
    return jax.shard_map(
        body,
        mesh=mesh,
        in_specs=(
            P(None, "dp", None),
            P(),
            P(None, None, "tp"),
            P(("dp", "tp"), None, None),
            P("dp", None, "tp"),
            P(None, "tp"),
            P(None, "tp"),
            P(None, "tp"),
            P(None, "tp"),
            P("tp"),
            P("tp"),
            P("tp"),
            P("dp", None, "tp"),
            P("dp", None, "tp"),
            P("dp", "tp", None, None),
            P("tp"),
            P("tp", None),
            P("tp", "dp"),
            P("tp", "dp"),
        ),
        out_specs=(P(None, "dp", "tp"), P("dp", "tp", None, None)),
        check_vma=False,
    )
```

```python
import jax
import jax.numpy as jnp
from jax import lax
from jax.experimental import pallas as pl
from jax.experimental.pallas import tpu as pltpu
from jax.sharding import PartitionSpec as P

G = 4
BLK = 128
LANES = 128
EPS = 1e-05
MESH = pl.DeviceIdType.MESH
F32 = jnp.float32
BF16 = jnp.bfloat16


def silu(v):
    return v / (1.0 + jnp.exp(-v))


def make_kernel(ndp, ntp, steps, rows, dc, lc, cb, heads, psize, nstate, gsz, feats, di):
    oc = feats // ntp
    ac = dc // ntp
    nchunk = lc // LANES
    hpc = LANES // psize
    small = cb + LANES
    rpd = dc // ntp

    def kernel(
        hid_hbm, gain_hbm, wdt_hbm, sc_hbm, so_hbm, ocodes_hbm, convx_hbm, convb_hbm, dtb_hbm,
        rate_hbm, skip_hbm, ng_hbm, hx0_hbm, hb0_hbm, state_hbm, codes_hbm, wzx_hbm, wbc_hbm,
        wout_hbm,
        out_ref, state_out,
        state, hx, hb, hrecv, s1, r1, s2, r2, cs, cr, gs, gr, qs, qr, os, orv, ags, agr, ms, mr,
        tbuf, rbuf, rv, wv, wz, wbc, wo,
        gain_ref, wdt_in, wdt_ref, sc_in, sc_ref, so_in, so_ref, ocodes_ref, convx_ref, convb_ref,
        dtb_ref, rate_ref, skip_ref, ng_ref, hx0_ref, hb0_ref, l_sems,
        w_sems, v_sem, st_sem, send_sem, h_sem, sem1, sem2, c_sem, g_sem, q_sem, o_sem, a_sem, m_sem,
    ):
        dp = lax.axis_index("dp")
        tp = lax.axis_index("tp")
        pending = []

        def send(src, dst, rsem, d, t):
            copy = pltpu.make_async_remote_copy(
                src_ref=src, dst_ref=dst, send_sem=send_sem, recv_sem=rsem,
                device_id=(d, t), device_id_type=MESH,
            )
            copy.start()
            pending.append(copy)

        def recv(src, dst, rsem):
            pltpu.make_async_remote_copy(
                src_ref=src, dst_ref=dst, send_sem=send_sem, recv_sem=rsem,
                device_id=(dp, tp), device_id_type=MESH,
            ).wait_recv()

        load = pltpu.make_async_copy(state_hbm, state, st_sem)
        load_w = pltpu.make_async_copy(wzx_hbm.at[pl.ds(dp * dc, dc)], wv, w_sems.at[0])
        load_w.start()
        load_own = pltpu.make_async_copy(
            codes_hbm.at[:, :, pl.ds(pl.multiple_of(tp * lc, LANES), lc)], rv.at[tp], w_sems.at[1]
        )
        load_own.start()
        load_bc = pltpu.make_async_copy(wbc_hbm.at[pl.ds(dp * dc, dc)], wbc, w_sems.at[2])
        load_bc.start()
        load_out = pltpu.make_async_copy(
            wout_hbm.at[:, pl.ds(pl.multiple_of(dp * dc, LANES), dc)], wo, w_sems.at[3]
        )
        load_out.start()
        load.start()

        def chunk(i):
            return pl.ds(pl.multiple_of(i * dc, LANES), dc)

        small_loads = [
            (gain_hbm.at[:, chunk(dp)], gain_ref), (wdt_hbm.at[:, chunk(dp)], wdt_in),
            (sc_hbm, sc_in), (so_hbm, so_in), (ocodes_hbm, ocodes_ref), (convx_hbm, convx_ref),
            (convb_hbm, convb_ref), (dtb_hbm, dtb_ref), (rate_hbm, rate_ref),
            (skip_hbm, skip_ref), (ng_hbm, ng_ref), (hx0_hbm, hx0_ref), (hb0_hbm, hb0_ref),
            (hid_hbm.at[:, :, chunk(dp)], hrecv.at[dp]),
        ]
        small_loads = [
            pltpu.make_async_copy(a, b, l_sems.at[i]) for i, (a, b) in enumerate(small_loads)
        ]
        for copy in small_loads:
            copy.start()

        barrier = pltpu.get_barrier_semaphore()
        for i in range(ndp):
            for j in range(ntp):
                if i + j > 0:
                    pl.semaphore_signal(
                        barrier, inc=1,
                        device_id=(lax.rem(dp + i, ndp), lax.rem(tp + j, ntp)),
                        device_id_type=MESH,
                    )
        pl.semaphore_wait(barrier, ndp * ntp - 1)

        for k in range(ntp - 1, 0, -1):
            peer = tp ^ k
            send(
                codes_hbm.at[:, :, pl.ds(pl.multiple_of(peer * lc, LANES), lc)],
                rv.at[tp], v_sem.at[k], dp, peer,
            )
        for k in range(1, ndp):
            peer = lax.rem(dp + k, ndp)
            send(hid_hbm.at[:, :, chunk(peer)], hrecv.at[dp], h_sem.at[k], peer, tp)
        for copy in small_loads:
            copy.wait()
        wdt_ref[...] = jnp.concatenate(
            [wdt_in[...].astype(F32), jnp.zeros((LANES - heads, dc), F32)], axis=0
        ).astype(BF16)
        for ref, table in ((sc_in, sc_ref), (so_in, so_ref)):
            power = jnp.exp2(ref[...].astype(F32))
            nrow, pair, ncol = power.shape
            for b in range(nrow):
                table[b] = jnp.concatenate(
                    [
                        jnp.broadcast_to(power[b, :, c : c + 1], (pair, BLK))
                        for c in range(ncol)
                    ],
                    axis=1,
                )
        hx[0:3] = hx0_ref[...].astype(F32)
        hb[0:3] = hb0_ref[...].astype(F32)
        for k in range(1, ndp):
            src = lax.rem(dp + ndp - k, ndp)
            recv(hrecv.at[src], hrecv.at[src], h_sem.at[k])

        load_out.wait()

        @pl.loop(0, lc // 32)
        def _(i):
            at = pl.ds(pl.multiple_of(i * 32, 32), 32)
            delta = ocodes_ref[at, :].astype(F32) * so_ref[i // (BLK // 32)]
            wo[at, :] = (wo[at, :].astype(F32) + delta).astype(BF16)

        load_w.wait()
        load_own.wait()
        load_bc.wait()
        for k in [0] + list(range(ntp - 1, 0, -1)):
            src = tp ^ k
            if k > 0:
                recv(rv.at[src], rv.at[src], v_sem.at[k])

            @pl.loop(0, rpd // 16)
            def _(i, src=src):
                first = src * rpd + i * 16
                code = rv[src, pl.ds(i * 16, 16)].astype(F32)
                old = wv[pl.ds(first, 16)].astype(F32)
                new = old + code * sc_ref[src * rpd // BLK][None]
                wz[pl.ds(pl.multiple_of(2 * first, 32), 32), :] = new.astype(BF16).reshape(32, lc)

        lane = lax.broadcasted_iota(jnp.int32, (rows, LANES), 1)
        lane_all = lax.broadcasted_iota(jnp.int32, (ndp * rows, LANES), 1)
        lane_sq = lax.broadcasted_iota(jnp.int32, (LANES, LANES), 1)
        put_row = lax.broadcasted_iota(jnp.int32, (LANES, 2 * LANES), 0)
        put_col = lax.broadcasted_iota(jnp.int32, (LANES, 2 * LANES), 1)
        owner = tp * oc // dc
        half = (tp * oc - owner * dc) // oc
        group = tp // gsz
        member = tp - group * gsz
        carried = None
        for s in range(steps):
            x = jnp.concatenate([hrecv[d, s].astype(F32) for d in range(ndp)], axis=0)
            if s > 0:
                x = x + carried
            ss = jnp.sum(x * x, axis=1, keepdims=True)
            y = (x * gain_ref[...]).astype(BF16)
            p = jnp.dot(y, wbc[...], preferred_element_type=F32)
            last = lax.dot_general(
                y, wdt_ref[...], (((1,), (1,)), ((), ())), preferred_element_type=F32
            )
            last = jnp.where(lane_all == LANES - 1, ss, last)
            for d in range(ndp):
                at = slice(d * rows, (d + 1) * rows)
                s1[s, d, :, :cb] = p[at]
                s1[s, d, :, cb:] = last[at]
            for k in range(1, ndp):
                peer = lax.rem(dp + k, ndp)
                send(s1.at[s, peer], r1.at[s, k], sem1.at[s, k], peer, tp)
            spread = []
            for half_of in range(2):
                place = (put_col == 2 * put_row + half_of).astype(BF16)
                parts = [
                    jnp.dot(y[:, c : c + LANES], place, preferred_element_type=F32).astype(BF16)
                    for c in range(0, dc, LANES)
                ]
                spread.append(jnp.concatenate(parts, axis=1))
            spread = jnp.concatenate(spread, axis=0)
            width = min(256, lc)
            for c in range(0, lc, width):
                p = jnp.dot(spread, wz[:, c : c + width], preferred_element_type=F32)
                for d in range(ndp):
                    s2[s, d, :, c : c + width] = p[d * rows : (d + 1) * rows].astype(BF16)
                    s2[s, d, :, lc + c : lc + c + width] = p[
                        (ndp + d) * rows : (ndp + d + 1) * rows
                    ].astype(BF16)
            for k in range(1, ndp):
                peer = lax.rem(dp + k, ndp)
                send(s2.at[s, peer], r2.at[s, k], sem2.at[s, k], peer, tp)
            for k in range(1, ndp):
                recv(s1.at[s, 0], r1.at[s, k], sem1.at[s, k])
            total = s1[s, dp]
            for k in range(1, ndp):
                total = total + r1[s, k]
            inv = lax.rsqrt(total[:, small - 1 :] / feats + EPS)
            hb[s + 3] = total[:, :cb] * inv
            mixed = convb_ref[4:5, :]
            for i in range(4):
                mixed = mixed + hb[s + i] * convb_ref[i : i + 1, :]
            piece = silu(mixed)
            cs[s] = piece
            cr[s, tp] = piece
            for k in range(1, ntp):
                send(cs.at[s], cr.at[s, tp], c_sem.at[s, k], dp, lax.rem(tp + k, ntp))
            z = total[:, cb : cb + heads] * inv + dtb_ref[...]
            dt = jnp.maximum(z, 0.0) + jnp.log1p(jnp.exp(-jnp.abs(z)))
            decay = jnp.exp(-dt * rate_ref[...])

            for k in range(1, ndp):
                recv(s2.at[s, 0], r2.at[s, k], sem2.at[s, k])
            inners = []
            for j in range(nchunk):
                at = slice(lc + j * LANES, lc + (j + 1) * LANES)
                here = slice(j * LANES, (j + 1) * LANES)
                v = s2[s, dp, :, at].astype(F32)
                for k in range(1, ndp):
                    v = v + r2[s, k, :, at].astype(F32)
                hx[s + 3, :, here] = v * inv
                mixed = convx_ref[4:5, here]
                for i in range(4):
                    mixed = mixed + hx[s + i, :, here] * convx_ref[i : i + 1, here]
                inner = silu(mixed)
                dte = jnp.zeros((rows, LANES), F32)
                dece = jnp.zeros((rows, LANES), F32)
                skip = jnp.zeros((rows, LANES), F32)
                for i in range(hpc):
                    h = j * hpc + i
                    inside = (lane >= i * psize) & (lane < (i + 1) * psize)
                    dte = jnp.where(inside, dt[:, h : h + 1], dte)
                    dece = jnp.where(inside, decay[:, h : h + 1], dece)
                    skip = jnp.where(inside, skip_ref[:, h : h + 1], skip)
                inners.append(skip * inner)
                tbuf[j, :rows] = dte * inner
                tbuf[j, rows:] = dece
            for k in range(1, ntp):
                src = lax.rem(tp + ntp - k, ntp)
                recv(cs.at[s], cr.at[s, src], c_sem.at[s, k])
            per = nstate // cb
            b0 = group * nstate // cb
            bmat = [cr[s, b0 + i] for i in range(per)]
            cmat = [cr[s, G * nstate // cb + b0 + i] for i in range(per)]
            bmat = bmat[0] if per == 1 else jnp.concatenate(bmat, axis=1)
            cmat = cmat[0] if per == 1 else jnp.concatenate(cmat, axis=1)
            if s == 0:
                load.wait()

            @pl.loop(0, nchunk, unroll=2)
            def _(j):
                full = jnp.concatenate(
                    [tbuf[j], jnp.zeros((LANES - 2 * rows, LANES), F32)], axis=0
                )
                flipped = full.T
                acc = jnp.zeros((LANES, LANES), F32)
                for r in range(rows):
                    new = (
                        flipped[:, rows + r : rows + r + 1] * state[r, j]
                        + flipped[:, r : r + 1] * bmat[r : r + 1, :]
                    )
                    state[r, j] = new
                    q = jnp.sum(new * cmat[r : r + 1, :], axis=1, keepdims=True)
                    acc = jnp.where(lane_sq == r, q, acc)
                rbuf[j] = acc.T[:rows]

            if s == steps - 1:
                store = pltpu.make_async_copy(state, state_out, st_sem)
                store.start()
            ss = jnp.zeros((rows, LANES), F32)
            for j in range(nchunk):
                here = slice(j * LANES, (j + 1) * LANES)
                v = s2[s, dp, :, here].astype(F32)
                for k in range(1, ndp):
                    v = v + r2[s, k, :, here].astype(F32)
                gated = (rbuf[j] + inners[j]) * silu(v * inv)
                ss = ss + gated * gated
                gs[s, :, here] = (gated * ng_ref[:, here]).astype(BF16)
            qs[s] = jnp.broadcast_to(jnp.sum(ss, axis=1, keepdims=True), (rows, LANES))
            gr[s, dp] = gs[s]
            qr[s, dp, member] = qs[s]
            for k in range(1, ndp):
                send(gs.at[s], gr.at[s, dp], g_sem.at[s, k], lax.rem(dp + k, ndp), tp)
            for k in range(ndp):
                for m in range(gsz):
                    if k + m > 0:
                        send(
                            qs.at[s], qr.at[s, dp, member], q_sem.at[s, k, m],
                            lax.rem(dp + k, ndp), group * gsz + lax.rem(member + m, gsz),
                        )
            for k in range(ndp):
                src = lax.rem(dp + ndp - k, ndp)
                if k > 0:
                    recv(gs.at[s], gr.at[s, src], g_sem.at[s, k])
                for m in range(gsz):
                    if k + m > 0:
                        frm = lax.rem(member + gsz - m, gsz)
                        recv(qs.at[s], qr.at[s, src, frm], q_sem.at[s, k, m])
            every = jnp.concatenate(
                [gr[s, d].astype(F32) for d in range(ndp)], axis=0
            ).astype(BF16)
            scales = []
            for d in range(ndp):
                sq = qr[s, d, 0]
                for m in range(1, gsz):
                    sq = sq + qr[s, d, m]
                scales.append(lax.rsqrt(sq[:, :1] / (di // G) + EPS))
            scale = jnp.concatenate(scales, axis=0)
            width = max(ac, min(256, dc))
            for c in range(0, dc, width):
                p = jnp.dot(every, wo[:, c : c + width], preferred_element_type=F32) * scale
                for i in range(width // ac):
                    os[s, c // ac + i] = p[:, i * ac : (i + 1) * ac].astype(BF16)
            for k in range(1, ntp):
                peer = lax.rem(tp + k, ntp)
                send(os.at[s, peer], orv.at[s, k], o_sem.at[s, k], dp, peer)
            for k in range(1, ntp):
                recv(os.at[s, 0], orv.at[s, k], o_sem.at[s, k])
            total = os[s, tp].astype(F32)
            for k in range(1, ntp):
                total = total + orv[s, k].astype(F32)
            total = total.astype(BF16)
            ags[s] = total
            agr[s, tp] = total
            for k in range(1, ntp):
                send(ags.at[s], agr.at[s, tp], a_sem.at[s, k], dp, lax.rem(tp + k, ntp))
            for k in range(1, ntp):
                src = lax.rem(tp + ntp - k, ntp)
                recv(ags.at[s], agr.at[s, src], a_sem.at[s, k])
            carried = jnp.concatenate([agr[s, t].astype(F32) for t in range(ntp)], axis=1)
            picked = carried[:, :oc]
            for i in range(1, dc // oc):
                picked = jnp.where(half == i, carried[:, i * oc : (i + 1) * oc], picked)
            for d in range(ndp):
                ms[s, d] = picked[d * rows : (d + 1) * rows].astype(BF16)

            @pl.when(owner == dp)
            def _():
                for k in range(1, ndp):
                    peer = lax.rem(dp + k, ndp)
                    pltpu.make_async_remote_copy(
                        src_ref=ms.at[s, peer], dst_ref=mr.at[s], send_sem=m_sem.at[s, 0],
                        recv_sem=m_sem.at[s, 1], device_id=(peer, tp), device_id_type=MESH,
                    ).start()

        store.wait()
        for s in range(steps):
            def final(s=s):
                return pltpu.make_async_remote_copy(
                    src_ref=ms.at[s, 0], dst_ref=mr.at[s], send_sem=m_sem.at[s, 0],
                    recv_sem=m_sem.at[s, 1], device_id=(dp, tp), device_id_type=MESH,
                )

            @pl.when(owner == dp)
            def _():
                out_ref[s] = ms[s, dp]
                for k in range(1, ndp):
                    final().wait_send()

            @pl.when(owner != dp)
            def _():
                final().wait_recv()
                out_ref[s] = mr[s]

        for copy in pending:
            copy.wait_send()

    vm = pltpu.VMEM
    scratch = [
        vm((rows, nchunk, LANES, nstate), F32),
        vm((steps + 3, rows, lc), F32),
        vm((steps + 3, rows, cb), F32),
        vm((ndp, steps, rows, dc), BF16),
        vm((steps, ndp, rows, small), F32),
        vm((steps, ndp, rows, small), F32),
        vm((steps, ndp, rows, 2 * lc), BF16),
        vm((steps, ndp, rows, 2 * lc), BF16),
        vm((steps, rows, cb), F32),
        vm((steps, ntp, rows, cb), F32),
        vm((steps, rows, lc), BF16),
        vm((steps, ndp, rows, lc), BF16),
        vm((steps, rows, LANES), F32),
        vm((steps, ndp, gsz, rows, LANES), F32),
        vm((steps, ntp, ndp * rows, ac), BF16),
        vm((steps, ntp, ndp * rows, ac), BF16),
        vm((steps, ndp * rows, ac), BF16),
        vm((steps, ntp, ndp * rows, ac), BF16),
        vm((steps, ndp, rows, oc), BF16),
        vm((steps, rows, oc), BF16),
        vm((nchunk, 2 * rows, LANES), F32),
        vm((nchunk, rows, LANES), F32),
        vm((ntp, rpd, 2, lc), BF16),
        vm((dc, 2, lc), BF16),
        vm((2 * dc, lc), BF16),
        vm((dc, cb), BF16),
        vm((lc, dc), BF16),
        vm((1, dc), F32),
        vm((heads, dc), BF16),
        vm((LANES, dc), BF16),
        vm((dc // BLK, 2, lc // BLK), jnp.int32),
        vm((dc // BLK, 2, lc), F32),
        vm((lc // BLK, 1, dc // BLK), jnp.int32),
        vm((lc // BLK, 1, dc), F32),
        vm((lc, dc), BF16),
        vm((5, lc), F32),
        vm((5, cb), F32),
        vm((1, heads), F32),
        vm((1, heads), F32),
        vm((1, heads), F32),
        vm((1, lc), F32),
        vm((3, rows, lc), BF16),
        vm((3, rows, cb), BF16),
        pltpu.SemaphoreType.DMA((14,)),
        pltpu.SemaphoreType.DMA((4,)),
        pltpu.SemaphoreType.DMA((ntp,)),
        pltpu.SemaphoreType.DMA(()),
        pltpu.SemaphoreType.DMA(()),
        pltpu.SemaphoreType.DMA((ndp,)),
        pltpu.SemaphoreType.DMA((steps, ndp)),
        pltpu.SemaphoreType.DMA((steps, ndp)),
        pltpu.SemaphoreType.DMA((steps, ntp)),
        pltpu.SemaphoreType.DMA((steps, ndp)),
        pltpu.SemaphoreType.DMA((steps, ndp, gsz)),
        pltpu.SemaphoreType.DMA((steps, ntp)),
        pltpu.SemaphoreType.DMA((steps, ntp)),
        pltpu.SemaphoreType.DMA((steps, 2)),
    ]
    vspec = pl.BlockSpec(memory_space=pltpu.VMEM)
    hspec = pl.BlockSpec(memory_space=pl.ANY)
    return pl.pallas_call(
        kernel,
        out_shape=(
            jax.ShapeDtypeStruct((steps, rows, oc), BF16),
            jax.ShapeDtypeStruct((rows, nchunk, LANES, nstate), F32),
        ),
        in_specs=[hspec] * 19,
        out_specs=(vspec, hspec),
        scratch_shapes=scratch,
        compiler_params=pltpu.CompilerParams(
            collective_id=0, has_side_effects=True, vmem_limit_bytes=60 * 1024 * 1024
        ),
    )


def body(
    hidden_in, pre_gain, w_zx, zx_codes, zx_exponents, w_bc, w_dt, conv_x, conv_bc, dt_bias,
    decay_rate, skip_gain, conv_state_x, conv_state_bc, ssm_state, norm_gain, w_out, out_codes,
    out_exponents,
):
    ndp, ntp = lax.axis_size("dp"), lax.axis_size("tp")
    steps, rows, feats = hidden_in.shape
    dc = feats // ndp
    lc = w_zx.shape[2]
    cb = w_bc.shape[1]
    _, heads, psize, nstate = ssm_state.shape
    gsz = ntp // G
    di = lc * ntp

    call = make_kernel(ndp, ntp, steps, rows, dc, lc, cb, heads, psize, nstate, gsz, feats, di)
    out, state = call(
        hidden_in, pre_gain[None], w_dt.T, zx_exponents, out_exponents[:, None], out_codes, conv_x,
        conv_bc, dt_bias[None], decay_rate[None], skip_gain[None], norm_gain[None],
        conv_state_x.transpose(1, 0, 2), conv_state_bc.transpose(1, 0, 2),
        ssm_state.reshape(rows, lc // LANES, LANES, nstate),
        zx_codes, w_zx, w_bc, w_out,
    )
    return out, state.reshape(ssm_state.shape)


def solution(mesh):
    return jax.shard_map(
        body,
        mesh=mesh,
        in_specs=(
            P(None, "dp", None),
            P(),
            P(None, None, "tp"),
            P(("dp", "tp"), None, None),
            P("dp", None, "tp"),
            P(None, "tp"),
            P(None, "tp"),
            P(None, "tp"),
            P(None, "tp"),
            P("tp"),
            P("tp"),
            P("tp"),
            P("dp", None, "tp"),
            P("dp", None, "tp"),
            P("dp", "tp", None, None),
            P("tp"),
            P("tp", None),
            P("tp", "dp"),
            P("tp", "dp"),
        ),
        out_specs=(P(None, "dp", "tp"), P("dp", "tp", None, None)),
        check_vma=False,
    )
```
